32 devices in a mesh: rows: 8 (over z, y), vecs: 4 (over x, core).
Axes of the slice: x: 2, y: 2, z: 4, core: 2. Of those that a mesh axis runs over, the one named last changes fastest.
Arguments:
- vectors: bfloat16 [24576, 512], P('rows', 'vecs'), may hold values from -8 to 8
- node_mass: float32 [24576], P('rows'), may hold values from 0.5 to 2
- cable_stiff: float32 [24576], P('rows'), may hold values from 0.1 to 1
- cable_nodes: int32 [8, 4], P('rows'), may hold values from 1 to 1152, 2304 in all within a row
- deck_rigidity: float32 [], replicated, may hold values from 0.3 to 1
- anchor_rows: int32 [8, 8, 4], P('rows'), may hold values from 0 to 3072, as said below
- anchor_stiff: float32 [8, 8, 4], P('rows'), may hold values from 0.2 to 1, as said below
- cut_low: float32 [], replicated, may hold values from 1.5 to 2.5
- top_bound: float32 [], replicated, may hold values from 7 to 9
Outputs:
- basis: bfloat16 [24576, 512], P('rows', 'vecs')
The draws below stay inside these ranges and needn't reach their ends.
Inputs may be any that keep to these rules, and one draw needn't show every extreme that they name: anchor_rows[r, q, s] is a node of partition r coupled through slot s to partition q, or 3072 where the slot is empty; slot s of r towards q is live exactly when slot s of q towards r is; live slots come first; no partition has live slots towards itself; a partition that is not a pylon partition has live slots only towards the partitions beside it in the cyclic order, which fill all 4 slots, and towards at most 4 pylon partitions; pylon partitions come in pairs half the cyclic order apart, and the two of a pair fill all 4 slots towards each other. anchor_stiff[r, q, s] equals anchor_stiff[q, r, s].
All inputs are finite; a program needn't handle non-finite values.
Results may differ from the reference program's by a relative error of at most 0.0072.
The reference program's roundings to bfloat16 on the way (of `filtered` and `factor`) count: a program that leaves them out, or rounds other values in their place, can miss the bound.
Values may be sent and summed in bfloat16 or wider, within the bound.
A program may use at most 64 MiB of HBM per device.

```python
import math
import jax
import jax.numpy as jnp
import numpy as np

ROWS_DEV = 3072
BLOCK = 512
SLOTS = 4
PYLONS = 4
CAB_DEV = 4
DECK_DEV = 768
CABLE_ROWS = 2304
CABLE_MOST = 1152
PIECES = 8
TOTAL = 24576


def draw_vectors(key, part):
    normal_draw = jax.random.normal(jax.random.fold_in(key, 21), (TOTAL, BLOCK), jnp.float32)
    mixed_draw = normal_draw + 0.6 * jnp.roll(normal_draw, 1, axis=1) + 0.4 * jnp.roll(normal_draw, 2, axis=1)
    heavy_parts = jax.random.permutation(jax.random.fold_in(key, 25), PIECES)[:4]
    owner_part = jnp.arange(TOTAL, dtype=jnp.int32) // ROWS_DEV
    is_heavy = jnp.any(owner_part[:, None] == heavy_parts[None, :], axis=1)
    part_scale = jnp.where(is_heavy, 2.8, 0.7)[:, None]
    mixed_draw = mixed_draw * part_scale
    return jnp.clip(mixed_draw, -8.0, 8.0).astype(jnp.bfloat16)


def anchor_counts(key):
    base_counts = jax.random.randint(jax.random.fold_in(key, 11), (PIECES, PIECES), 1, SLOTS + 1)
    first_index = jnp.arange(PIECES)[:, None]
    second_index = jnp.arange(PIECES)[None, :]
    half_count = PIECES // 2
    pair_base = jax.random.permutation(jax.random.fold_in(key, 14), half_count)[:PYLONS // 2]
    pylon_list = jnp.concatenate([pair_base, pair_base + half_count])
    pick = jax.random.randint(jax.random.fold_in(key, 15), (PIECES,), 0, PYLONS)
    partner = pylon_list[pick]
    linked = partner[:, None] == second_index
    linked = linked | linked.T
    symmetric = jnp.where(first_index < second_index, base_counts, base_counts.T)
    symmetric = jnp.where(linked, symmetric, 0)
    is_pylon = jnp.any(jnp.arange(PIECES)[:, None] == pylon_list[None, :], axis=1)
    opposite = (second_index == (first_index + half_count) % PIECES) & is_pylon[:, None]
    symmetric = jnp.where(opposite, SLOTS, symmetric)
    neighbour = (second_index == (first_index + 1) % PIECES) | (first_index == (second_index + 1) % PIECES)
    symmetric = jnp.where(neighbour, SLOTS, symmetric)
    return jnp.where(first_index == second_index, 0, symmetric)


def draw_anchor_rows(key, part):
    counts = anchor_counts(key)
    picked_rows = jax.random.randint(jax.random.fold_in(key, 12), (PIECES, PIECES, SLOTS), 0, ROWS_DEV)
    live_slots = jnp.arange(SLOTS)[None, None, :] < counts[:, :, None]
    return jnp.where(live_slots, picked_rows, ROWS_DEV).astype(jnp.int32)


def draw_anchor_stiff(key, part):
    spring_draw = jnp.exp(jax.random.uniform(jax.random.fold_in(key, 13), (PIECES, PIECES, SLOTS), jnp.float32, math.log(0.2), 0.0))
    first_index = jnp.arange(PIECES)[:, None, None]
    second_index = jnp.arange(PIECES)[None, :, None]
    symmetric = jnp.where(first_index < second_index, spring_draw, jnp.transpose(spring_draw, (1, 0, 2)))
    return symmetric.astype(jnp.float32)


def levels(key, dims, pieces, smallest, top_value):
    gain = 1.0
    for dim, parts in pieces:
        steps = jax.random.uniform(jax.random.fold_in(jax.random.fold_in(key, 6), dim), (parts,), jnp.float32, smallest / len(pieces), top_value / len(pieces))
        gain = gain * jnp.repeat(jnp.exp(steps), dims[dim] // parts).reshape((-1,) + (1,) * (len(dims) - 1 - dim))
    return gain


def length_profile(amount, total, bound, slope):
    portions = [(1 << 20) // math.isqrt(rank ** slope) + 1 for rank in range(2, amount + 1)]
    rest, given = total - bound - (amount - 1), [1] * (amount - 1)
    while rest > 0:
        candidates = [i for i in range(amount - 1) if given[i] < bound]
        pool, budget = sum([portions[i] for i in candidates]), rest
        for i in candidates:
            addition = min(bound - given[i], max(1, budget * portions[i] // pool), rest)
            given[i] = given[i] + addition
            rest = rest - addition
    return np.array([bound] + given)


def ragged(key, count, total, limit, slope):
    if count == 2:
        one = jax.random.randint(key, (), max(1, total - limit), min(limit, total - 1) + 1)
        return jnp.stack([one, total - one])
    tallies = jnp.asarray(length_profile(count, total, limit, slope), jnp.int32)
    couples = (count - 1) // 2
    donor, sink = tallies[1:1 + 2 * couples:2], tallies[2:2 + 2 * couples:2]
    room = jnp.minimum(donor - 1, limit - sink)
    passed = jax.random.randint(jax.random.fold_in(key, 1), (couples,), 0, 1 << 20) % (room + 1)
    tallies = tallies.at[1:1 + 2 * couples:2].set(donor - passed).at[2:2 + 2 * couples:2].set(sink + passed)
    return tallies[jax.random.permutation(jax.random.fold_in(key, 2), count)]


def setup_inputs(seed: int = 0) -> dict:
    seeds = jax.random.split(jax.random.key(seed), 10)
    vectors = draw_vectors(jax.random.fold_in(seeds[9], 71), 0)
    node_mass = jnp.clip(jnp.exp(math.log(2.0) - 1.3862944 * jax.random.uniform(seeds[1], (TOTAL,), jnp.float32) ** levels(seeds[1], (TOTAL,), ((0, 8),), -0.2, 0.2)), 0.5, 2.0)
    cable_stiff = jnp.clip(jnp.exp(math.log(1.0) - 2.3025851 * jax.random.uniform(seeds[2], (TOTAL,), jnp.float32) ** levels(seeds[2], (TOTAL,), ((0, 8),), -0.2, 0.2)), 0.1, 1.0)
    cable_nodes = jax.vmap(lambda own: ragged(own, CAB_DEV, CABLE_ROWS, CABLE_MOST, 2))(jax.random.split(seeds[3], PIECES)).reshape((PIECES, CAB_DEV)).astype(jnp.int32)
    deck_rigidity = jnp.clip(jax.random.uniform(seeds[4], (), jnp.float32, 0.3, 1.0), 0.3, 1.0)
    anchor_rows = draw_anchor_rows(jax.random.fold_in(seeds[9], 71), 0)
    anchor_stiff = draw_anchor_stiff(jax.random.fold_in(seeds[9], 71), 0)
    cut_low = jnp.clip(jax.random.uniform(seeds[7], (), jnp.float32, 1.5, 2.5), 1.5, 2.5)
    top_bound = jnp.clip(jax.random.uniform(seeds[8], (), jnp.float32, 7.0, 9.0), 7.0, 9.0)
    return {"vectors": vectors, "node_mass": node_mass, "cable_stiff": cable_stiff, "cable_nodes": cable_nodes, "deck_rigidity": deck_rigidity, "anchor_rows": anchor_rows, "anchor_stiff": anchor_stiff, "cut_low": cut_low, "top_bound": top_bound}


def cable_term(values, stiff_rows, cable_nodes):
    cable_ends = jnp.cumsum(cable_nodes, axis=1)
    positions = jnp.arange(CABLE_ROWS - 1, dtype=jnp.int32) + 1
    breaks = jnp.any(positions[None, :, None] == cable_ends[:, None, :], axis=2)
    cable_links = jnp.where(breaks, jnp.zeros_like(stiff_rows[:, :CABLE_ROWS - 1]), stiff_rows[:, :CABLE_ROWS - 1])
    cable_flux = cable_links[:, :, None] * (values[:, :-1] - values[:, 1:])
    return jnp.pad(cable_flux, ((0, 0), (0, 1), (0, 0))) - jnp.pad(cable_flux, ((0, 0), (1, 0), (0, 0)))

def deck_term(values, deck_rigidity):
    chain = values.reshape(PIECES * DECK_DEV, values.shape[2])
    deck_flux = deck_rigidity * (chain[:-1] - chain[1:])
    result = jnp.pad(deck_flux, ((0, 1), (0, 0))) - jnp.pad(deck_flux, ((1, 0), (0, 0)))
    return result.reshape(PIECES, DECK_DEV, values.shape[2])

def anchor_term(values, anchor_rows, anchor_stiff):
    part_index = jnp.arange(PIECES, dtype=jnp.int32)
    remote_rows = jnp.transpose(anchor_rows, (1, 0, 2))
    remote_values = values.at[part_index[None, :, None], remote_rows].get(mode='fill', fill_value=0.0)
    local_values = values.at[part_index[:, None, None], anchor_rows].get(mode='fill', fill_value=0.0)
    anchor_force = anchor_stiff[:, :, :, None] * (local_values - remote_values)
    owners = jnp.broadcast_to(part_index[:, None, None], anchor_rows.shape)
    return jnp.zeros_like(values).at[owners, anchor_rows].add(anchor_force, mode='drop')

def operate(values, mass_rows, stiff_rows, cable_nodes, deck_rigidity, anchor_rows, anchor_stiff):
    cable_side = cable_term(values[:, :CABLE_ROWS], stiff_rows, cable_nodes)
    deck_side = deck_term(values[:, CABLE_ROWS:], deck_rigidity)
    springs = jnp.concatenate([cable_side, deck_side], axis=1)
    return mass_rows[:, :, None] * values + springs + anchor_term(values, anchor_rows, anchor_stiff)

def reference(vectors, node_mass, cable_stiff, cable_nodes, deck_rigidity, anchor_rows, anchor_stiff, cut_low, top_bound):
    mass_rows = node_mass.reshape(PIECES, ROWS_DEV)
    stiff_rows = cable_stiff.reshape(PIECES, ROWS_DEV)
    start_block = vectors.astype(jnp.float32).reshape(PIECES, ROWS_DEV, BLOCK)
    center = (top_bound + cut_low) * 0.5
    half_width = (top_bound - cut_low) * 0.5

    def apply_operator(values):
        return operate(values, mass_rows, stiff_rows, cable_nodes, deck_rigidity, anchor_rows, anchor_stiff)
    first_degree = (apply_operator(start_block) - center * start_block) / half_width
    second_degree = 2.0 * (apply_operator(first_degree) - center * first_degree) / half_width - start_block
    filtered = second_degree.reshape(TOTAL, BLOCK).astype(jnp.bfloat16)
    gram_matrix = jnp.dot(filtered.T.astype(jnp.float32), filtered.astype(jnp.float32), preferred_element_type=jnp.float32) / TOTAL
    lower_factor = jnp.linalg.cholesky(gram_matrix)
    identity = jnp.eye(BLOCK, dtype=jnp.float32)
    inverse = jax.scipy.linalg.solve_triangular(lower_factor, identity, lower=True)
    factor = inverse.T.astype(jnp.bfloat16)
    return jnp.dot(filtered.astype(jnp.float32), factor.astype(jnp.float32), preferred_element_type=jnp.float32).astype(jnp.bfloat16)
```

```python
import jax
import jax.numpy as jnp
from jax import lax
from jax.experimental import pallas as pl
from jax.experimental.pallas import tpu as pltpu
from jax.sharding import PartitionSpec as P

CABLE_ROWS = 2304
NB = 128
HI = lax.Precision.HIGHEST


def eliminate(block):
    lane = lax.broadcasted_iota(jnp.int32, (8, NB), 1)
    sub = lax.broadcasted_iota(jnp.int32, (8, NB), 0)
    tiles = NB // 8
    left = [block[8 * t : 8 * t + 8, :] for t in range(tiles)]
    right = [jnp.where(lane == sub + 8 * t, 1.0, 0.0).astype(jnp.float32) for t in range(tiles)]
    for j in range(NB):
        home, row = divmod(j, 8)
        pivot_row = left[home][row : row + 1, :]
        scale = lax.rsqrt(pivot_row[:, j : j + 1])
        scaled = pivot_row * scale
        inverse_row = right[home][row : row + 1, :] * scale
        scaled_all = jnp.broadcast_to(scaled, (8, NB))
        inverse_all = jnp.broadcast_to(inverse_row, (8, NB))
        for t in range(home, tiles):
            column = jnp.broadcast_to(left[t][:, j : j + 1], (8, NB)) * scale
            if t == home:
                below = sub > row
                left[t] = jnp.where(below, left[t] - column * scaled_all, left[t])
                right[t] = jnp.where(
                    below, right[t] - column * inverse_all, jnp.where(sub == row, inverse_all, right[t])
                )
            else:
                left[t] = left[t] - column * scaled_all
                right[t] = right[t] - column * inverse_all
    return jnp.concatenate(right, axis=0)


def mm(a, b, dims):
    return lax.dot_general(a, b, (dims, ((), ())), precision=HI, preferred_element_type=jnp.float32)


def inverse_factor(gram_ref, inv_ref):
    size = gram_ref.shape[0]
    inv_ref[...] = jnp.zeros_like(inv_ref)
    for k in range(size // NB):
        lo, hi = k * NB, (k + 1) * NB
        diag_inv = eliminate(gram_ref[lo:hi, lo:hi])
        if k:
            inv_ref[lo:hi, :lo] = mm(diag_inv, inv_ref[lo:hi, :lo], ((1,), (0,)))
        inv_ref[lo:hi, lo:hi] = diag_inv
        if hi < size:
            panel = mm(gram_ref[hi:, lo:hi], diag_inv, ((1,), (1,)))
            for i in range(hi, size, NB):
                part = panel[i - hi : i - hi + NB]
                gram_ref[i : i + NB, hi : i + NB] -= mm(part, panel[: i - hi + NB], ((1,), (1,)))
            inv_ref[hi:, :hi] -= mm(panel, inv_ref[lo:hi, :hi], ((1,), (0,)))


def inverse_kernel(gram_in, out, gram_ref):
    gram_ref[...] = gram_in[...]
    inverse_factor(gram_ref, out)


def with_halo(block, sides, width):
    for axis, dim in sides:
        count = lax.axis_size(axis)
        forward = [(i, i + 1) for i in range(count - 1)]
        backward = [(target, source) for source, target in forward]
        low = lax.ppermute(
            lax.slice_in_dim(block, block.shape[dim] - width, None, axis=dim), axis, forward
        )
        high = lax.ppermute(lax.slice_in_dim(block, 0, width, axis=dim), axis, backward)
        block = jnp.concatenate([low, block, high], axis=dim)
    return block


def body(
    vectors,
    node_mass,
    cable_stiff,
    cable_nodes,
    deck_rigidity,
    anchor_rows,
    anchor_stiff,
    cut_low,
    top_bound,
):
    part_count = lax.axis_size("rows")
    my_index = lax.axis_index("rows")
    own_width = vectors.shape[1]
    cable_ends = jnp.cumsum(cable_nodes[0])
    positions = jnp.arange(CABLE_ROWS - 1, dtype=jnp.int32) + 1
    breaks = jnp.any(positions[:, None] == cable_ends[None, :], axis=1)
    cable_links = jnp.where(breaks, 0.0, cable_stiff[: CABLE_ROWS - 1])[:, None]
    left_open = jnp.where(my_index > 0, deck_rigidity, 0.0)
    right_open = jnp.where(my_index < part_count - 1, deck_rigidity, 0.0)
    slot_rows = anchor_rows[0]
    slot_stiff = anchor_stiff[0][:, :, None]
    flat_rows = slot_rows.reshape(-1)

    def apply_operator(values):
        cable_part = values[:CABLE_ROWS]
        deck_part = values[CABLE_ROWS:]
        cable_flux = cable_links * (cable_part[:-1] - cable_part[1:])
        cable_side = jnp.pad(cable_flux, ((0, 1), (0, 0))) - jnp.pad(cable_flux, ((1, 0), (0, 0)))
        outgoing = jnp.take(values, slot_rows, axis=0, mode="fill", fill_value=0.0)
        incoming = lax.all_to_all(
            outgoing.astype(jnp.bfloat16), "rows", split_axis=0, concat_axis=0, tiled=True
        ).astype(outgoing.dtype)
        padded = with_halo(deck_part.astype(jnp.bfloat16), (("rows", 0),), 1).astype(
            deck_part.dtype
        )
        before_row = padded[0]
        after_row = padded[-1]
        deck_flux = deck_rigidity * (deck_part[:-1] - deck_part[1:])
        first_flux = left_open * (before_row - deck_part[0])
        last_flux = right_open * (deck_part[-1] - after_row)
        deck_side = jnp.concatenate([deck_flux, last_flux[None, :]], axis=0) - jnp.concatenate(
            [first_flux[None, :], deck_flux], axis=0
        )
        anchor_force = (slot_stiff * (outgoing - incoming)).reshape(-1, values.shape[1])
        anchor_side = jnp.zeros_like(values).at[flat_rows].add(anchor_force, mode="drop")
        springs = jnp.concatenate([cable_side, deck_side], axis=0)
        return node_mass[:, None] * values + springs + anchor_side

    start_block = vectors.astype(jnp.float32)
    center = (top_bound + cut_low) * 0.5
    half_width = (top_bound - cut_low) * 0.5
    first_degree = (apply_operator(start_block) - center * start_block) / half_width
    second_degree = (
        2.0 * (apply_operator(first_degree) - center * first_degree) / half_width - start_block
    )
    filtered = second_degree.astype(jnp.bfloat16)
    columns = lax.all_gather(filtered, "vecs", axis=1, tiled=True)
    total_rows = filtered.shape[0] * part_count
    gram_whole = jnp.einsum("rb,rc->bc", columns, columns, preferred_element_type=jnp.float32)
    gram_matrix = lax.psum(gram_whole, "rows") / total_rows
    size = gram_matrix.shape[0]
    inverse = pl.pallas_call(
        inverse_kernel,
        out_shape=jax.ShapeDtypeStruct((size, size), jnp.float32),
        in_specs=[pl.BlockSpec(memory_space=pltpu.VMEM)],
        out_specs=pl.BlockSpec(memory_space=pltpu.VMEM),
        scratch_shapes=[pltpu.VMEM((size, size), jnp.float32)],
    )(gram_matrix)
    factor = inverse.T.astype(jnp.bfloat16)
    own_factor = lax.dynamic_slice_in_dim(factor, lax.axis_index("vecs") * own_width, own_width, 1)
    return jnp.dot(columns, own_factor, preferred_element_type=jnp.float32).astype(jnp.bfloat16)


def solution(mesh):
    return jax.shard_map(
        body,
        mesh=mesh,
        in_specs=(
            P("rows", "vecs"),
            P("rows"),
            P("rows"),
            P("rows", None),
            P(),
            P("rows", None, None),
            P("rows", None, None),
            P(),
            P(),
        ),
        out_specs=P("rows", "vecs"),
        check_vma=False,
    )
```

```python
import functools

import jax
import jax.numpy as jnp
from jax import lax
from jax.experimental import pallas as pl
from jax.experimental.pallas import tpu as pltpu
from jax.sharding import PartitionSpec as P

CABLE_ROWS = 2304
MESH = pl.DeviceIdType.MESH
PAD = 8

NB = 128
HI = lax.Precision.HIGHEST


def eliminate(block):
    lane = lax.broadcasted_iota(jnp.int32, (8, NB), 1)
    sub = lax.broadcasted_iota(jnp.int32, (8, NB), 0)
    tiles = NB // 8
    left = [block[8 * t : 8 * t + 8, :] for t in range(tiles)]
    right = [jnp.where(lane == sub + 8 * t, 1.0, 0.0).astype(jnp.float32) for t in range(tiles)]
    for j in range(NB):
        home, row = divmod(j, 8)
        pivot_row = left[home][row : row + 1, :]
        scale = lax.rsqrt(pivot_row[:, j : j + 1])
        scaled = pivot_row * scale
        inverse_row = right[home][row : row + 1, :] * scale
        scaled_all = jnp.broadcast_to(scaled, (8, NB))
        inverse_all = jnp.broadcast_to(inverse_row, (8, NB))
        for t in range(home, tiles):
            column = jnp.broadcast_to(left[t][:, j : j + 1], (8, NB)) * scale
            if t == home:
                below = sub > row
                left[t] = jnp.where(below, left[t] - column * scaled_all, left[t])
                right[t] = jnp.where(
                    below, right[t] - column * inverse_all, jnp.where(sub == row, inverse_all, right[t])
                )
            else:
                left[t] = left[t] - column * scaled_all
                right[t] = right[t] - column * inverse_all
    return jnp.concatenate(right, axis=0)


def mm(a, b, dims):
    return lax.dot_general(a, b, (dims, ((), ())), precision=HI, preferred_element_type=jnp.float32)


def inverse_factor(gram_ref, inv_ref):
    size = gram_ref.shape[0]
    inv_ref[...] = jnp.zeros_like(inv_ref)
    for k in range(size // NB):
        lo, hi = k * NB, (k + 1) * NB
        diag_inv = eliminate(gram_ref[lo:hi, lo:hi])
        if k:
            inv_ref[lo:hi, :lo] = mm(diag_inv, inv_ref[lo:hi, :lo], ((1,), (0,)))
        inv_ref[lo:hi, lo:hi] = diag_inv
        if hi < size:
            panel = mm(gram_ref[hi:, lo:hi], diag_inv, ((1,), (1,)))
            for i in range(hi, size, NB):
                part = panel[i - hi : i - hi + NB]
                gram_ref[i : i + NB, hi : i + NB] -= mm(part, panel[: i - hi + NB], ((1,), (1,)))
            inv_ref[hi:, :hi] -= mm(panel, inv_ref[lo:hi, :hi], ((1,), (0,)))


def split_three(value):
    high = value.astype(jnp.bfloat16)
    rest = value - high.astype(jnp.float32)
    middle = rest.astype(jnp.bfloat16)
    low = (rest - middle.astype(jnp.float32)).astype(jnp.bfloat16)
    return jnp.concatenate([high, middle, low], axis=0)


def kernel(
    parts,
    splits,
    x_ref,
    mass_ref,
    stiff_ref,
    nodes_ref,
    rigid_ref,
    rows_ref,
    spring_ref,
    low_ref,
    top_ref,
    target_ref,
    out_ref,
    value_ref,
    first_ref,
    link_ref,
    diag_ref,
    hot_ref,
    force_ref,
    send_buf,
    recv_buf,
    cols_ref,
    sum_ref,
    half_ref,
    piece_ref,
    all_ref,
    gram_ref,
    inv_ref,
    ex_send,
    ex_recv,
    quarter_send,
    quarter_recv,
    fold_send,
    fold_recv,
    piece_send,
    piece_recv,
    give_send,
    give_recv,
    grow_send,
    grow_recv,
):
    me = lax.axis_index("rows")
    col = lax.axis_index("vecs")
    count, width = x_ref.shape
    slots = rows_ref.shape[1]
    total_rows = count * parts

    barrier = pltpu.get_barrier_semaphore()
    for k in range(1, splits):
        pl.semaphore_signal(
            barrier, inc=1, device_id=(me, lax.rem(col + k, splits)), device_id_type=MESH
        )

    def greet(k, carry):
        pl.semaphore_signal(
            barrier, inc=1, device_id=(lax.rem(me + k, parts), col), device_id_type=MESH
        )
        return carry

    lax.fori_loop(1, parts, greet, 0)
    pl.semaphore_wait(barrier, parts - 1 + splits - 1)

    top = jnp.full((1, width), top_ref[0], jnp.float32)
    bottom = jnp.full((1, width), low_ref[0], jnp.float32)
    center = (top + bottom) * 0.5
    inverse_half = 1.0 / ((top - bottom) * 0.5)

    chunk = count // splits
    zero_pad = jnp.zeros((PAD, width), jnp.float32)
    for ref in (value_ref, first_ref, link_ref):
        ref[0:PAD, :] = zero_pad
        ref[PAD + count :, :] = zero_pad
    for lo in range(0, count, chunk):
        value_ref[PAD + lo : PAD + lo + chunk, :] = x_ref[lo : lo + chunk, :].astype(jnp.float32)

    def remote(turn, k, target):
        return pltpu.make_async_remote_copy(
            src_ref=send_buf.at[turn, target],
            dst_ref=recv_buf.at[turn, me],
            send_sem=ex_send.at[turn, k],
            recv_sem=ex_recv.at[turn, k],
            device_id=(target, col),
            device_id_type=MESH,
        )

    def arrival(turn, k):
        source = lax.rem(me + parts - k, parts)
        return pltpu.make_async_remote_copy(
            src_ref=send_buf.at[turn, source],
            dst_ref=recv_buf.at[turn, source],
            send_sem=ex_send.at[turn, k],
            recv_sem=ex_recv.at[turn, k],
            device_id=(source, col),
            device_id_type=MESH,
        )

    unroll = parts <= 8

    def send_anchors(turn, ref):
        first_row = ref[PAD + CABLE_ROWS : PAD + CABLE_ROWS + 1, :]
        last_row = ref[PAD + count - 1 : PAD + count, :]
        blank = jnp.zeros((8 - slots - 2, width), jnp.float32)

        def pick(q, carry):
            picked = [
                ref[pl.ds(PAD + jnp.minimum(rows_ref[q, s], count - 1), 1), :] for s in range(slots)
            ]
            send_buf[turn, q] = jnp.concatenate(picked + [first_row, last_row, blank], axis=0)
            return carry

        lax.fori_loop(0, parts, pick, 0, unroll=unroll)

        def push(k, carry):
            remote(turn, k, lax.rem(me + k, parts)).start()
            return carry

        lax.fori_loop(1, parts, push, 0, unroll=unroll)
        recv_buf[turn, me] = send_buf[turn, me]

    def collect(turn, scale):
        def take(k, carry):
            arrival(turn, k).wait_recv()
            return carry

        lax.fori_loop(1, parts, take, 0, unroll=unroll)

        def pull(q, carry):
            difference = send_buf[turn, q] - recv_buf[turn, q]
            for s in range(slots):
                live = jnp.where(rows_ref[q, s] < count, spring_ref[q, s], 0.0)
                force_ref[pl.ds(q * slots + s, 1), :] = live * difference[s : s + 1, :]
            return carry

        lax.fori_loop(0, parts, pull, 0, unroll=unroll)
        before = recv_buf[turn, lax.rem(me + parts - 1, parts)]
        after = recv_buf[turn, lax.rem(me + 1, parts)]
        own = send_buf[turn, me]
        left_open = jnp.where(me > 0, rigid_ref[0], 0.0)
        right_open = jnp.where(me < parts - 1, rigid_ref[0], 0.0)
        edge = jnp.concatenate(
            [
                left_open * (own[slots : slots + 1] - before[slots + 1 : slots + 2]),
                right_open * (own[slots + 1 : slots + 2] - after[slots : slots + 1]),
                jnp.zeros((6, width), jnp.float32),
            ],
            axis=0,
        )
        force_ref[parts * slots : parts * slots + 8, :] = edge
        return split_three(force_ref[...] * scale)

    send_anchors(0, value_ref)

    lane = lax.broadcasted_iota(jnp.int32, (1, width), 1)
    rigid = rigid_ref[0]
    cuts = []
    running = nodes_ref[0, 0]
    for j in range(1, nodes_ref.shape[1]):
        cuts.append(running)
        running = running + nodes_ref[0, j]
    cuts.append(running)
    for r in range(count // width):
        place = lane + r * width
        open_link = place < CABLE_ROWS - 1
        for cut in cuts:
            open_link = open_link & (place + 1 != cut)
        deck_link = (place >= CABLE_ROWS) & (place < count - 1)
        link = jnp.where(open_link, stiff_ref[r : r + 1, :], jnp.where(deck_link, rigid, 0.0))
        lo = PAD + r * width
        link_ref[lo : lo + width, :] = jnp.broadcast_to(link, (width, width)).T
        mass = mass_ref[r : r + 1, :] - center
        diag_ref[r * width : (r + 1) * width, :] = jnp.broadcast_to(mass, (width, width)).T

    def base(ref, lo):
        at = PAD + lo
        here = ref[at : at + chunk, :]
        down = link_ref[at : at + chunk, :] * (here - ref[at + 1 : at + chunk + 1, :])
        up = link_ref[at - 1 : at + chunk - 1, :] * (here - ref[at - 1 : at + chunk - 1, :])
        return diag_ref[lo : lo + chunk, :] * here + down + up

    for lo in range(0, count, chunk):
        first_ref[PAD + lo : PAD + lo + chunk, :] = base(value_ref, lo) * inverse_half
        node = lax.broadcasted_iota(jnp.int32, (chunk, target_ref.shape[1]), 0) + lo
        hot_ref[lo : lo + chunk, :] = jnp.where(node == target_ref[...], 1.0, 0.0).astype(jnp.bfloat16)

    pulls = collect(0, inverse_half)
    for lo in range(0, count, chunk):
        first_ref[PAD + lo : PAD + lo + chunk, :] += jnp.dot(
            hot_ref[lo : lo + chunk, :], pulls, preferred_element_type=jnp.float32
        )
    send_anchors(1, first_ref)
    double = 2.0 * inverse_half
    for lo in range(0, count, chunk):
        diag_ref[lo : lo + chunk, :] = (
            base(first_ref, lo) * double - value_ref[PAD + lo : PAD + lo + chunk, :]
        )
    pulls = collect(1, double)
    for lo in range(0, count, chunk):
        cols_ref[col, lo : lo + chunk, :] = (
            diag_ref[lo : lo + chunk, :]
            + jnp.dot(hot_ref[lo : lo + chunk, :], pulls, preferred_element_type=jnp.float32)
        ).astype(jnp.bfloat16)

    def share(owner, target, piece, k, i):
        rows = pl.ds(pl.multiple_of(piece * chunk, chunk), chunk)
        return pltpu.make_async_remote_copy(
            src_ref=cols_ref.at[owner, rows],
            dst_ref=cols_ref.at[owner, rows],
            send_sem=quarter_send.at[k, i],
            recv_sem=quarter_recv.at[k, i],
            device_id=(me, target),
            device_id_type=MESH,
        )

    for k in range(1, splits):
        target = lax.rem(col + k, splits)
        share(col, target, target, k, 0).start()
    for k in range(1, splits):
        share(lax.rem(col + splits - k, splits), col, col, k, 0).wait_recv()

    mine = pl.ds(pl.multiple_of(col * chunk, chunk), chunk)
    packed = jnp.concatenate([cols_ref[b, mine, :] for b in range(splits)], axis=1)
    for i in range(splits):
        rows = lax.dot_general(
            packed[:, i * width : (i + 1) * width],
            packed[:, : (i + 1) * width],
            (((0,), (0,)), ((), ())),
            preferred_element_type=jnp.float32,
        )
        for j in range(i + 1):
            at = (i * (i + 1) // 2 + j) * width
            sum_ref[at : at + width, :] = rows[:, j * width : (j + 1) * width]
    length = sum_ref.shape[0]
    used = splits * (splits + 1) // 2 * width
    if used < length:
        sum_ref[used:, :] = jnp.zeros((length - used, width), jnp.float32)

    bits = splits.bit_length() - 1
    start = 0
    offset = 0
    for b in range(bits):
        half = length >> (b + 1)
        bit = lax.rem(col // (1 << b), 2)
        partner = col + (1 << b) * (1 - 2 * bit)
        landing = half_ref.at[pl.ds(offset, half)]
        copy = pltpu.make_async_remote_copy(
            src_ref=sum_ref.at[pl.ds(pl.multiple_of(start + (1 - bit) * half, 8), half)],
            dst_ref=landing,
            send_sem=fold_send.at[b],
            recv_sem=fold_recv.at[b],
            device_id=(me, partner),
            device_id_type=MESH,
        )
        copy.start()
        copy.wait()
        start = pl.multiple_of(start + bit * half, 8)
        sum_ref[pl.ds(start, half), :] += half_ref[offset : offset + half, :]
        offset += half
    part = length // splits
    unit = part // parts

    def piece(q):
        return pl.ds(pl.multiple_of(start + q * unit, 8), unit)

    def send_piece(k, carry):
        target = lax.rem(me + k, parts)
        pltpu.make_async_remote_copy(
            src_ref=sum_ref.at[piece(target)],
            dst_ref=piece_ref.at[me],
            send_sem=piece_send.at[k],
            recv_sem=piece_recv.at[k],
            device_id=(target, col),
            device_id_type=MESH,
        ).start()
        return carry

    def piece_copy(k):
        source = lax.rem(me + parts - k, parts)
        return pltpu.make_async_remote_copy(
            src_ref=sum_ref.at[piece(source)],
            dst_ref=piece_ref.at[source],
            send_sem=piece_send.at[k],
            recv_sem=piece_recv.at[k],
            device_id=(source, col),
            device_id_type=MESH,
        )

    lax.fori_loop(1, parts, send_piece, 0, unroll=unroll)

    def add_piece(k, total):
        piece_copy(k).wait_recv()
        return total + piece_ref[lax.rem(me + parts - k, parts)]

    all_ref[piece(me), :] = lax.fori_loop(1, parts, add_piece, sum_ref[piece(me), :], unroll=unroll)

    def give(owner, target, k):
        return pltpu.make_async_remote_copy(
            src_ref=all_ref.at[piece(owner)],
            dst_ref=all_ref.at[piece(owner)],
            send_sem=give_send.at[k],
            recv_sem=give_recv.at[k],
            device_id=(target, col),
            device_id_type=MESH,
        )

    def give_start(k, carry):
        give(me, lax.rem(me + k, parts), k).start()
        return carry

    def give_wait(k, carry):
        give(lax.rem(me + parts - k, parts), me, k).wait_recv()
        return carry

    lax.fori_loop(1, parts, give_start, 0, unroll=unroll)
    lax.fori_loop(1, parts, give_wait, 0, unroll=unroll)
    grown = []
    held = part
    for b in reversed(range(bits)):
        bit = lax.rem(col // (1 << b), 2)
        partner = col + (1 << b) * (1 - 2 * bit)

        def grow(at):
            rows = pl.ds(pl.multiple_of(at, 8), held)
            return pltpu.make_async_remote_copy(
                src_ref=all_ref.at[rows],
                dst_ref=all_ref.at[rows],
                send_sem=grow_send.at[b],
                recv_sem=grow_recv.at[b],
                device_id=(me, partner),
                device_id_type=MESH,
            )

        copy = grow(start)
        copy.start()
        grown.append(copy)
        grow(start + (1 - 2 * bit) * held).wait_recv()
        start = start - bit * held
        held = 2 * held

    for k in range(1, splits):
        target = lax.rem(col + k, splits)
        for i in range(1, splits):
            share(col, target, lax.rem(target + i, splits), k, i).start()

    for i in range(splits):
        for j in range(i + 1):
            at = (i * (i + 1) // 2 + j) * width
            gram_ref[i * width : (i + 1) * width, j * width : (j + 1) * width] = all_ref[
                at : at + width, :
            ] * (1.0 / total_rows)
    inverse_factor(gram_ref, inv_ref)

    for k in range(1, splits):
        for i in range(1, splits):
            share(lax.rem(col + splits - k, splits), col, lax.rem(col + i, splits), k, i).wait_recv()
    factor = inv_ref[pl.ds(pl.multiple_of(col * width, width), width), :].astype(jnp.bfloat16)
    for lo in range(0, count, chunk):
        block = jnp.concatenate([cols_ref[b, lo : lo + chunk, :] for b in range(splits)], axis=1)
        out_ref[lo : lo + chunk, :] = lax.dot_general(
            block, factor, (((1,), (1,)), ((), ())), preferred_element_type=jnp.float32
        ).astype(jnp.bfloat16)

    for k in range(1, splits):
        target = lax.rem(col + k, splits)
        for i in range(splits):
            share(col, target, lax.rem(target + i, splits), k, i).wait_send()
    for copy in grown:
        copy.wait_send()

    def settle(k, carry):
        target = lax.rem(me + k, parts)
        remote(0, k, target).wait_send()
        remote(1, k, target).wait_send()
        piece_copy(k).wait_send()
        give(me, target, k).wait_send()
        return carry

    lax.fori_loop(1, parts, settle, 0, unroll=unroll)


def body(
    parts,
    splits,
    vectors,
    node_mass,
    cable_stiff,
    cable_nodes,
    deck_rigidity,
    anchor_rows,
    anchor_stiff,
    cut_low,
    top_bound,
):
    count, width = vectors.shape
    slots = anchor_rows.shape[2]
    places = jnp.concatenate(
        [
            anchor_rows.reshape(1, -1),
            jnp.array([[CABLE_ROWS, count - 1] + [count] * 6], jnp.int32),
        ],
        axis=1,
    )
    targets = jnp.tile(places, (1, 3))
    size = splits * width
    blocks = splits * (splits + 1) // 2
    unit = -(-(blocks * width) // (splits * parts * 8)) * 8
    length = unit * parts * splits
    bits = splits.bit_length() - 1
    vmem = pl.BlockSpec(memory_space=pltpu.VMEM)
    smem = pl.BlockSpec(memory_space=pltpu.SMEM)
    sem = pltpu.SemaphoreType.DMA
    f32 = jnp.float32
    return pl.pallas_call(
        functools.partial(kernel, parts, splits),
        out_shape=jax.ShapeDtypeStruct((count, width), jnp.bfloat16),
        in_specs=[vmem, vmem, vmem, smem, smem, smem, smem, smem, smem, vmem],
        out_specs=vmem,
        scratch_shapes=[
            pltpu.VMEM((count + 2 * PAD, width), f32),
            pltpu.VMEM((count + 2 * PAD, width), f32),
            pltpu.VMEM((count + 2 * PAD, width), f32),
            pltpu.VMEM((count, width), f32),
            pltpu.VMEM((count, targets.shape[1]), jnp.bfloat16),
            pltpu.VMEM((places.shape[1], width), f32),
            pltpu.VMEM((2, parts, 8, width), f32),
            pltpu.VMEM((2, parts, 8, width), f32),
            pltpu.VMEM((splits, count, width), jnp.bfloat16),
            pltpu.VMEM((length, width), f32),
            pltpu.VMEM((length, width), f32),
            pltpu.VMEM((parts, unit, width), f32),
            pltpu.VMEM((length, width), f32),
            pltpu.VMEM((size, size), f32),
            pltpu.VMEM((size, size), f32),
            sem((2, parts)),
            sem((2, parts)),
            sem((splits, splits)),
            sem((splits, splits)),
            sem((bits,)),
            sem((bits,)),
            sem((parts,)),
            sem((parts,)),
            sem((parts,)),
            sem((parts,)),
            sem((bits,)),
            sem((bits,)),
        ],
        compiler_params=pltpu.CompilerParams(
            collective_id=0, has_side_effects=True, vmem_limit_bytes=60 * 1024 * 1024
        ),
    )(
        vectors,
        node_mass.reshape(-1, width),
        cable_stiff.reshape(-1, width),
        cable_nodes,
        deck_rigidity.reshape(1),
        anchor_rows.reshape(-1, slots),
        anchor_stiff.reshape(-1, slots),
        cut_low.reshape(1),
        top_bound.reshape(1),
        targets,
    )


def solution(mesh):
    return jax.shard_map(
        functools.partial(body, mesh.shape["rows"], mesh.shape["vecs"]),
        mesh=mesh,
        in_specs=(
            P("rows", "vecs"),
            P("rows"),
            P("rows"),
            P("rows", None),
            P(),
            P("rows", None, None),
            P("rows", None, None),
            P(),
            P(),
        ),
        out_specs=P("rows", "vecs"),
        check_vma=False,
    )
```

```python
import functools

import jax
import jax.numpy as jnp
from jax import lax
from jax.experimental import pallas as pl
from jax.experimental.pallas import tpu as pltpu
from jax.sharding import PartitionSpec as P

CABLE_ROWS = 2304
MESH = pl.DeviceIdType.MESH
PAD = 8


NB = 128
HI = lax.Precision.HIGHEST


def spread(tile, lane):
    return jnp.broadcast_to(tile[:, lane : lane + 1], tile.shape)


def eliminate(block):
    lane = lax.broadcasted_iota(jnp.int32, (8, NB), 1)
    sub = lax.broadcasted_iota(jnp.int32, (8, NB), 0)
    tiles = NB // 8
    left = [block[8 * t : 8 * t + 8, :] for t in range(tiles)]
    right = [jnp.where(lane == sub + 8 * t, 1.0, 0.0).astype(jnp.float32) for t in range(tiles)]
    for g in range(tiles):
        home, away = left[g], right[g]
        column = [spread(home, 8 * g + i) for i in range(8)]
        scales, rows = [], []
        for i in range(8):
            scale = lax.rsqrt(column[i][i : i + 1, :])
            scales.append(scale)
            column[i] = column[i] * scale
            rows.append([column[i][n : n + 1, :] for n in range(8)])
            for n in range(i + 1, 8):
                column[n] = column[n] - column[i] * rows[i][n]
        for i in range(8):
            upper = home[i : i + 1, :] * scales[i]
            inverse = away[i : i + 1, :] * scales[i]
            home = jnp.where(sub > i, home - column[i] * upper, jnp.where(sub == i, upper, home))
            away = jnp.where(sub > i, away - column[i] * inverse, jnp.where(sub == i, inverse, away))
        right[g] = away
        for t in range(g + 1, tiles):
            factor = [spread(left[t], 8 * g + i) for i in range(8)]
            for i in range(8):
                factor[i] = factor[i] * scales[i]
                for n in range(i + 1, 8):
                    factor[n] = factor[n] - factor[i] * rows[i][n]
            for i in range(8):
                left[t] = left[t] - factor[i] * home[i : i + 1, :]
                right[t] = right[t] - factor[i] * away[i : i + 1, :]
    return jnp.concatenate(right, axis=0)


def mm(a, b, dims):
    return lax.dot_general(a, b, (dims, ((), ())), precision=HI, preferred_element_type=jnp.float32)


def inverse_factor(gram_ref, inv_ref, between):
    size = gram_ref.shape[0]
    inv_ref[...] = jnp.zeros_like(inv_ref)
    for k in range(size // NB):
        lo, hi = k * NB, (k + 1) * NB
        diag_inv = eliminate(gram_ref[lo:hi, lo:hi])
        if k == (size // NB - 1) // 2:
            between()
        if k:
            inv_ref[lo:hi, :lo] = mm(diag_inv, inv_ref[lo:hi, :lo], ((1,), (0,)))
        inv_ref[lo:hi, lo:hi] = diag_inv
        if hi < size:
            panel = mm(gram_ref[hi:, lo:hi], diag_inv, ((1,), (1,)))
            for i in range(hi, size, NB):
                part = panel[i - hi : i - hi + NB]
                gram_ref[i : i + NB, hi : i + NB] -= mm(part, panel[: i - hi + NB], ((1,), (1,)))
            inv_ref[hi:, :hi] -= mm(panel, inv_ref[lo:hi, :hi], ((1,), (0,)))


def travel_plan(splits):
    if splits != 4:
        direct = [
            (block, target, block, piece)
            for target in range(splits)
            for block in range(target)
            for piece in range(splits)
            if piece != target
        ]
        return direct, []
    first = [(0, 2, 0, 0), (0, 3, 0, 1), (1, 2, 1, 0), (1, 3, 1, 1)]
    first += [(2, 3, 0, 2), (2, 3, 1, 2), (3, 2, 0, 3), (3, 2, 1, 3)]
    first += [(0, 1, 0, 0), (0, 1, 0, 2), (0, 1, 0, 3), (2, 3, 2, 0), (2, 3, 2, 1), (2, 3, 2, 2)]
    second = [(2, 3, 0, 0), (2, 3, 1, 0), (3, 2, 0, 1), (3, 2, 1, 1)]
    return first, second


def split_three(value):
    high = value.astype(jnp.bfloat16)
    rest = value - high.astype(jnp.float32)
    middle = rest.astype(jnp.bfloat16)
    low = (rest - middle.astype(jnp.float32)).astype(jnp.bfloat16)
    return jnp.concatenate([high, middle, low], axis=0)


def kernel(
    parts,
    splits,
    x_ref,
    mass_ref,
    stiff_ref,
    nodes_ref,
    rigid_ref,
    rows_ref,
    spring_ref,
    low_ref,
    top_ref,
    out_ref,
    value_ref,
    first_ref,
    link_ref,
    diag_ref,
    hot_ref,
    force_ref,
    send_buf,
    recv_buf,
    cols_ref,
    sum_ref,
    half_ref,
    piece_ref,
    all_ref,
    gram_ref,
    inv_ref,
    ex_send,
    ex_recv,
    quarter_send,
    quarter_recv,
    travel_send,
    travel_recv,
    fold_send,
    fold_recv,
    piece_send,
    piece_recv,
    give_send,
    give_recv,
    grow_send,
    grow_recv,
):
    me = lax.axis_index("rows")
    col = lax.axis_index("vecs")
    count, width = x_ref.shape
    slots = rows_ref.shape[2]
    total_rows = count * parts

    barrier = pltpu.get_barrier_semaphore()
    for k in range(1, splits):
        pl.semaphore_signal(
            barrier, inc=1, device_id=(me, lax.rem(col + k, splits)), device_id_type=MESH
        )

    def greet(k, carry):
        pl.semaphore_signal(
            barrier, inc=1, device_id=(lax.rem(me + k, parts), col), device_id_type=MESH
        )
        return carry

    lax.fori_loop(1, parts, greet, 0)
    pl.semaphore_wait(barrier, parts - 1 + splits - 1)

    top = jnp.full((1, width), top_ref[0], jnp.float32)
    bottom = jnp.full((1, width), low_ref[0], jnp.float32)
    center = (top + bottom) * 0.5
    inverse_half = 1.0 / ((top - bottom) * 0.5)

    chunk = count // splits
    zero_pad = jnp.zeros((PAD, width), jnp.float32)
    for ref in (value_ref, first_ref, link_ref):
        ref[0:PAD, :] = zero_pad
        ref[PAD + count :, :] = zero_pad
    for lo in range(0, count, chunk):
        value_ref[PAD + lo : PAD + lo + chunk, :] = x_ref[lo : lo + chunk, :].astype(jnp.float32)

    def remote(turn, k, target):
        return pltpu.make_async_remote_copy(
            src_ref=send_buf.at[turn, target],
            dst_ref=recv_buf.at[turn, me],
            send_sem=ex_send.at[turn, k],
            recv_sem=ex_recv.at[turn, k],
            device_id=(target, col),
            device_id_type=MESH,
        )

    def arrival(turn, k):
        source = lax.rem(me + parts - k, parts)
        return pltpu.make_async_remote_copy(
            src_ref=send_buf.at[turn, source],
            dst_ref=recv_buf.at[turn, source],
            send_sem=ex_send.at[turn, k],
            recv_sem=ex_recv.at[turn, k],
            device_id=(source, col),
            device_id_type=MESH,
        )

    unroll = parts <= 8

    def send_anchors(turn, ref):
        first_row = ref[PAD + CABLE_ROWS : PAD + CABLE_ROWS + 1, :]
        last_row = ref[PAD + count - 1 : PAD + count, :]
        blank = jnp.zeros((8 - slots - 2, width), jnp.float32)

        def pick(q, carry):
            picked = [
                ref[pl.ds(PAD + jnp.minimum(rows_ref[0, q, s], count - 1), 1), :] for s in range(slots)
            ]
            send_buf[turn, q] = jnp.concatenate(picked + [first_row, last_row, blank], axis=0)
            return carry

        lax.fori_loop(0, parts, pick, 0, unroll=unroll)

        def push(k, carry):
            remote(turn, k, lax.rem(me + k, parts)).start()
            return carry

        lax.fori_loop(1, parts, push, 0, unroll=unroll)
        recv_buf[turn, me] = send_buf[turn, me]

    def collect(turn, scale):
        def take(k, carry):
            arrival(turn, k).wait_recv()
            return carry

        lax.fori_loop(1, parts, take, 0, unroll=unroll)

        def pull(q, carry):
            difference = send_buf[turn, q] - recv_buf[turn, q]
            for s in range(slots):
                live = jnp.where(rows_ref[0, q, s] < count, spring_ref[0, q, s], 0.0)
                force_ref[pl.ds(q * slots + s, 1), :] = live * difference[s : s + 1, :]
            return carry

        lax.fori_loop(0, parts, pull, 0, unroll=unroll)
        before = recv_buf[turn, lax.rem(me + parts - 1, parts)]
        after = recv_buf[turn, lax.rem(me + 1, parts)]
        own = send_buf[turn, me]
        left_open = jnp.where(me > 0, rigid_ref[0], 0.0)
        right_open = jnp.where(me < parts - 1, rigid_ref[0], 0.0)
        edge = jnp.concatenate(
            [
                left_open * (own[slots : slots + 1] - before[slots + 1 : slots + 2]),
                right_open * (own[slots + 1 : slots + 2] - after[slots : slots + 1]),
                jnp.zeros((6, width), jnp.float32),
            ],
            axis=0,
        )
        force_ref[parts * slots : parts * slots + 8, :] = edge
        return split_three(force_ref[...] * scale)

    send_anchors(0, value_ref)

    forces = force_ref.shape[0]
    order = lax.rem(lax.broadcasted_iota(jnp.int32, (1, 3 * forces), 1), forces)
    ends = parts * slots
    target = jnp.where(order == ends, CABLE_ROWS, jnp.where(order == ends + 1, count - 1, count))

    def place_anchor(q, carry):
        for s in range(slots):
            carry = jnp.where(order == q * slots + s, rows_ref[0, q, s], carry)
        return carry

    target = lax.fori_loop(0, parts, place_anchor, target, unroll=unroll)

    lane = lax.broadcasted_iota(jnp.int32, (1, width), 1)
    rigid = rigid_ref[0]
    cuts = []
    running = nodes_ref[0, 0]
    for j in range(1, nodes_ref.shape[1]):
        cuts.append(running)
        running = running + nodes_ref[0, j]
    cuts.append(running)
    for r in range(count // width):
        place = lane + r * width
        open_link = place < CABLE_ROWS - 1
        for cut in cuts:
            open_link = open_link & (place + 1 != cut)
        deck_link = (place >= CABLE_ROWS) & (place < count - 1)
        link = jnp.where(open_link, stiff_ref[r : r + 1, :], jnp.where(deck_link, rigid, 0.0))
        lo = PAD + r * width
        link_ref[lo : lo + width, :] = jnp.broadcast_to(link, (width, width)).T
        mass = mass_ref[r : r + 1, :] - center
        diag_ref[r * width : (r + 1) * width, :] = jnp.broadcast_to(mass, (width, width)).T

    def base(ref, lo):
        at = PAD + lo
        here = ref[at : at + chunk, :]
        down = link_ref[at : at + chunk, :] * (here - ref[at + 1 : at + chunk + 1, :])
        up = link_ref[at - 1 : at + chunk - 1, :] * (here - ref[at - 1 : at + chunk - 1, :])
        return diag_ref[lo : lo + chunk, :] * here + down + up

    for lo in range(0, count, chunk):
        first_ref[PAD + lo : PAD + lo + chunk, :] = base(value_ref, lo) * inverse_half
        node = lax.broadcasted_iota(jnp.int32, (chunk, 3 * forces), 0) + lo
        hot_ref[lo : lo + chunk, :] = jnp.where(node == target, 1.0, 0.0).astype(jnp.bfloat16)

    pulls = collect(0, inverse_half)
    for lo in range(0, count, chunk):
        first_ref[PAD + lo : PAD + lo + chunk, :] += jnp.dot(
            hot_ref[lo : lo + chunk, :], pulls, preferred_element_type=jnp.float32
        )
    send_anchors(1, first_ref)
    double = 2.0 * inverse_half
    for lo in range(0, count, chunk):
        diag_ref[lo : lo + chunk, :] = (
            base(first_ref, lo) * double - value_ref[PAD + lo : PAD + lo + chunk, :]
        )
    pulls = collect(1, double)
    for lo in range(0, count, chunk):
        cols_ref[col, lo : lo + chunk, :] = (
            diag_ref[lo : lo + chunk, :]
            + jnp.dot(hot_ref[lo : lo + chunk, :], pulls, preferred_element_type=jnp.float32)
        ).astype(jnp.bfloat16)

    def share(owner, target, piece, k):
        rows = pl.ds(pl.multiple_of(piece * chunk, chunk), chunk)
        return pltpu.make_async_remote_copy(
            src_ref=cols_ref.at[owner, rows],
            dst_ref=cols_ref.at[owner, rows],
            send_sem=quarter_send.at[k],
            recv_sem=quarter_recv.at[k],
            device_id=(me, target),
            device_id_type=MESH,
        )

    for k in range(1, splits):
        target = lax.rem(col + k, splits)
        share(col, target, target, k).start()
    for k in range(1, splits):
        share(lax.rem(col + splits - k, splits), col, col, k).wait_recv()

    mine = pl.ds(pl.multiple_of(col * chunk, chunk), chunk)
    packed = jnp.concatenate([cols_ref[b, mine, :] for b in range(splits)], axis=1)
    for i in range(splits):
        rows = lax.dot_general(
            packed[:, i * width : (i + 1) * width],
            packed[:, : (i + 1) * width],
            (((0,), (0,)), ((), ())),
            preferred_element_type=jnp.float32,
        )
        for j in range(i + 1):
            at = (i * (i + 1) // 2 + j) * width
            sum_ref[at : at + width, :] = rows[:, j * width : (j + 1) * width]
    length = sum_ref.shape[0]
    used = splits * (splits + 1) // 2 * width
    if used < length:
        sum_ref[used:, :] = jnp.zeros((length - used, width), jnp.float32)

    bits = splits.bit_length() - 1
    start = 0
    offset = 0
    for b in range(bits):
        half = length >> (b + 1)
        bit = lax.rem(col // (1 << b), 2)
        partner = col + (1 << b) * (1 - 2 * bit)
        landing = half_ref.at[pl.ds(offset, half)]
        copy = pltpu.make_async_remote_copy(
            src_ref=sum_ref.at[pl.ds(pl.multiple_of(start + (1 - bit) * half, 8), half)],
            dst_ref=landing,
            send_sem=fold_send.at[b],
            recv_sem=fold_recv.at[b],
            device_id=(me, partner),
            device_id_type=MESH,
        )
        copy.start()
        copy.wait()
        start = pl.multiple_of(start + bit * half, 8)
        sum_ref[pl.ds(start, half), :] += half_ref[offset : offset + half, :]
        offset += half
    part = length // splits
    unit = part // parts

    def piece(q):
        return pl.ds(pl.multiple_of(start + q * unit, 8), unit)

    def send_piece(k, carry):
        target = lax.rem(me + k, parts)
        pltpu.make_async_remote_copy(
            src_ref=sum_ref.at[piece(target)],
            dst_ref=piece_ref.at[me],
            send_sem=piece_send.at[k],
            recv_sem=piece_recv.at[k],
            device_id=(target, col),
            device_id_type=MESH,
        ).start()
        return carry

    def piece_copy(k):
        source = lax.rem(me + parts - k, parts)
        return pltpu.make_async_remote_copy(
            src_ref=sum_ref.at[piece(source)],
            dst_ref=piece_ref.at[source],
            send_sem=piece_send.at[k],
            recv_sem=piece_recv.at[k],
            device_id=(source, col),
            device_id_type=MESH,
        )

    lax.fori_loop(1, parts, send_piece, 0, unroll=unroll)

    def add_piece(k, total):
        piece_copy(k).wait_recv()
        return total + piece_ref[lax.rem(me + parts - k, parts)]

    all_ref[piece(me), :] = lax.fori_loop(1, parts, add_piece, sum_ref[piece(me), :], unroll=unroll)

    def give(owner, target, k):
        return pltpu.make_async_remote_copy(
            src_ref=all_ref.at[piece(owner)],
            dst_ref=all_ref.at[piece(owner)],
            send_sem=give_send.at[k],
            recv_sem=give_recv.at[k],
            device_id=(target, col),
            device_id_type=MESH,
        )

    def give_start(k, carry):
        give(me, lax.rem(me + k, parts), k).start()
        return carry

    def give_wait(k, carry):
        give(lax.rem(me + parts - k, parts), me, k).wait_recv()
        return carry

    lax.fori_loop(1, parts, give_start, 0, unroll=unroll)
    lax.fori_loop(1, parts, give_wait, 0, unroll=unroll)
    grown = []
    held = part
    for b in reversed(range(bits)):
        bit = lax.rem(col // (1 << b), 2)
        partner = col + (1 << b) * (1 - 2 * bit)

        def grow(at):
            rows = pl.ds(pl.multiple_of(at, 8), held)
            return pltpu.make_async_remote_copy(
                src_ref=all_ref.at[rows],
                dst_ref=all_ref.at[rows],
                send_sem=grow_send.at[b],
                recv_sem=grow_recv.at[b],
                device_id=(me, partner),
                device_id_type=MESH,
            )

        copy = grow(start)
        copy.start()
        grown.append(copy)
        grow(start + (1 - 2 * bit) * held).wait_recv()
        start = start - bit * held
        held = 2 * held

    first_trips, second_trips = travel_plan(splits)

    def trip(number):
        _, target, block, piece = (first_trips + second_trips)[number]
        rows = pl.ds(piece * chunk, chunk)
        return pltpu.make_async_remote_copy(
            src_ref=cols_ref.at[block, rows],
            dst_ref=cols_ref.at[block, rows],
            send_sem=travel_send.at[number],
            recv_sem=travel_recv.at[number],
            device_id=(me, target),
            device_id_type=MESH,
        )

    def each_trip(numbers, end, act):
        trips = first_trips + second_trips
        for device in range(splits):
            own = [n for n in numbers if trips[n][end] == device]
            if own:

                @pl.when(col == device)
                def _():
                    for n in own:
                        act(trip(n))

    early = range(len(first_trips))
    late = range(len(first_trips), len(first_trips) + len(second_trips))
    each_trip(early, 0, lambda copy: copy.start())

    def pass_on():
        each_trip(early, 1, lambda copy: copy.wait_recv())
        each_trip(late, 0, lambda copy: copy.start())

    for i in range(splits):
        for j in range(i + 1):
            at = (i * (i + 1) // 2 + j) * width
            gram_ref[i * width : (i + 1) * width, j * width : (j + 1) * width] = all_ref[
                at : at + width, :
            ] * (1.0 / total_rows)
    inverse_factor(gram_ref, inv_ref, pass_on)
    each_trip(late, 1, lambda copy: copy.wait_recv())

    for device in range(splits):

        @pl.when(col == device)
        def _():
            used_width = (device + 1) * width
            factor = inv_ref[device * width : used_width, :used_width].astype(jnp.bfloat16)
            for lo in range(0, count, chunk):
                block = jnp.concatenate(
                    [cols_ref[b, lo : lo + chunk, :] for b in range(device + 1)], axis=1
                )
                out_ref[lo : lo + chunk, :] = lax.dot_general(
                    block, factor, (((1,), (1,)), ((), ())), preferred_element_type=jnp.float32
                ).astype(jnp.bfloat16)

    for k in range(1, splits):
        target = lax.rem(col + k, splits)
        share(col, target, target, k).wait_send()
    each_trip(range(len(first_trips) + len(second_trips)), 0, lambda copy: copy.wait_send())
    for copy in grown:
        copy.wait_send()

    def settle(k, carry):
        target = lax.rem(me + k, parts)
        remote(0, k, target).wait_send()
        remote(1, k, target).wait_send()
        piece_copy(k).wait_send()
        give(me, target, k).wait_send()
        return carry

    lax.fori_loop(1, parts, settle, 0, unroll=unroll)


def body(
    parts,
    splits,
    vectors,
    node_mass,
    cable_stiff,
    cable_nodes,
    deck_rigidity,
    anchor_rows,
    anchor_stiff,
    cut_low,
    top_bound,
):
    count, width = vectors.shape
    slots = anchor_rows.shape[2]
    forces = parts * slots + 8
    trips = sum(len(trips) for trips in travel_plan(splits))
    size = splits * width
    blocks = splits * (splits + 1) // 2
    unit = -(-(blocks * width) // (splits * parts * 8)) * 8
    length = unit * parts * splits
    bits = splits.bit_length() - 1
    vmem = pl.BlockSpec(memory_space=pltpu.VMEM)
    smem = pl.BlockSpec(memory_space=pltpu.SMEM)
    sem = pltpu.SemaphoreType.DMA
    f32 = jnp.float32
    return pl.pallas_call(
        functools.partial(kernel, parts, splits),
        out_shape=jax.ShapeDtypeStruct((count, width), jnp.bfloat16),
        in_specs=[vmem, vmem, vmem, smem, smem, smem, smem, smem, smem],
        out_specs=vmem,
        scratch_shapes=[
            pltpu.VMEM((count + 2 * PAD, width), f32),
            pltpu.VMEM((count + 2 * PAD, width), f32),
            pltpu.VMEM((count + 2 * PAD, width), f32),
            pltpu.VMEM((count, width), f32),
            pltpu.VMEM((count, 3 * forces), jnp.bfloat16),
            pltpu.VMEM((forces, width), f32),
            pltpu.VMEM((2, parts, 8, width), f32),
            pltpu.VMEM((2, parts, 8, width), f32),
            pltpu.VMEM((splits, count, width), jnp.bfloat16),
            pltpu.VMEM((length, width), f32),
            pltpu.VMEM((length, width), f32),
            pltpu.VMEM((parts, unit, width), f32),
            pltpu.VMEM((length, width), f32),
            pltpu.VMEM((size, size), f32),
            pltpu.VMEM((size, size), f32),
            sem((2, parts)),
            sem((2, parts)),
            sem((splits,)),
            sem((splits,)),
            sem((trips,)),
            sem((trips,)),
            sem((bits,)),
            sem((bits,)),
            sem((parts,)),
            sem((parts,)),
            sem((parts,)),
            sem((parts,)),
            sem((bits,)),
            sem((bits,)),
        ],
        compiler_params=pltpu.CompilerParams(
            collective_id=0, has_side_effects=True, vmem_limit_bytes=60 * 1024 * 1024
        ),
    )(
        vectors,
        node_mass.reshape(-1, width),
        cable_stiff.reshape(-1, width),
        cable_nodes,
        deck_rigidity.reshape(1),
        anchor_rows,
        anchor_stiff,
        cut_low.reshape(1),
        top_bound.reshape(1),
    )


def solution(mesh):
    return jax.shard_map(
        functools.partial(body, mesh.shape["rows"], mesh.shape["vecs"]),
        mesh=mesh,
        in_specs=(
            P("rows", "vecs"),
            P("rows"),
            P("rows"),
            P("rows", None),
            P(),
            P("rows", None, None),
            P("rows", None, None),
            P(),
            P(),
        ),
        out_specs=P("rows", "vecs"),
        check_vma=False,
    )
```

```python
import functools

import jax
import jax.numpy as jnp
from jax import lax
from jax.experimental import pallas as pl
from jax.experimental.pallas import tpu as pltpu
from jax.sharding import PartitionSpec as P

CABLE_ROWS = 2304
MESH = pl.DeviceIdType.MESH
PAD = 8


NB = 128
HI = lax.Precision.HIGHEST


def spread(tile, lane):
    return jnp.broadcast_to(tile[:, lane : lane + 1], tile.shape)


def eliminate(block):
    lane = lax.broadcasted_iota(jnp.int32, (8, NB), 1)
    sub = lax.broadcasted_iota(jnp.int32, (8, NB), 0)
    tiles = NB // 8
    left = [block[8 * t : 8 * t + 8, :] for t in range(tiles)]
    right = [jnp.where(lane == sub + 8 * t, 1.0, 0.0).astype(jnp.float32) for t in range(tiles)]
    for g in range(tiles):
        home, away = left[g], right[g]
        column = [spread(home, 8 * g + i) for i in range(8)]
        scales, rows = [], []
        for i in range(8):
            scale = lax.rsqrt(column[i][i : i + 1, :])
            scales.append(scale)
            column[i] = column[i] * scale
            rows.append([column[i][n : n + 1, :] for n in range(8)])
            for n in range(i + 1, 8):
                column[n] = column[n] - column[i] * rows[i][n]
        for i in range(8):
            upper = home[i : i + 1, :] * scales[i]
            inverse = away[i : i + 1, :] * scales[i]
            home = jnp.where(sub > i, home - column[i] * upper, jnp.where(sub == i, upper, home))
            away = jnp.where(sub > i, away - column[i] * inverse, jnp.where(sub == i, inverse, away))
        right[g] = away
        for t in range(g + 1, tiles):
            factor = [spread(left[t], 8 * g + i) for i in range(8)]
            for i in range(8):
                factor[i] = factor[i] * scales[i]
                for n in range(i + 1, 8):
                    factor[n] = factor[n] - factor[i] * rows[i][n]
            for i in range(8):
                left[t] = left[t] - factor[i] * home[i : i + 1, :]
                right[t] = right[t] - factor[i] * away[i : i + 1, :]
    return jnp.concatenate(right, axis=0)


def mm(a, b, dims):
    return lax.dot_general(a, b, (dims, ((), ())), precision=HI, preferred_element_type=jnp.float32)


def inverse_factor(gram_ref, inv_ref, between):
    size = gram_ref.shape[0]
    inv_ref[...] = jnp.zeros_like(inv_ref)
    for k in range(size // NB):
        lo, hi = k * NB, (k + 1) * NB
        diag_inv = eliminate(gram_ref[lo:hi, lo:hi])
        if k == (size // NB - 1) // 2:
            between()
        if k:
            inv_ref[lo:hi, :lo] = mm(diag_inv, inv_ref[lo:hi, :lo], ((1,), (0,)))
        inv_ref[lo:hi, lo:hi] = diag_inv
        if hi < size:
            panel = mm(gram_ref[hi:, lo:hi], diag_inv, ((1,), (1,)))
            for i in range(hi, size, NB):
                part = panel[i - hi : i - hi + NB]
                gram_ref[i : i + NB, hi : i + NB] -= mm(part, panel[: i - hi + NB], ((1,), (1,)))
            inv_ref[hi:, :hi] -= mm(panel, inv_ref[lo:hi, :hi], ((1,), (0,)))


def travel_plan(splits):
    if splits != 4:
        direct = [
            (block, target, block, piece)
            for target in range(splits)
            for block in range(target)
            for piece in range(splits)
            if piece != target
        ]
        return direct, []
    first = [(0, 2, 0, 0), (0, 3, 0, 1), (1, 2, 1, 0), (1, 3, 1, 1)]
    first += [(2, 3, 0, 2), (2, 3, 1, 2), (3, 2, 0, 3), (3, 2, 1, 3)]
    first += [(0, 1, 0, 0), (0, 1, 0, 2), (0, 1, 0, 3), (2, 3, 2, 0), (2, 3, 2, 1), (2, 3, 2, 2)]
    second = [(2, 3, 0, 0), (2, 3, 1, 0), (3, 2, 0, 1), (3, 2, 1, 1)]
    return first, second


def split_three(value):
    high = value.astype(jnp.bfloat16)
    rest = value - high.astype(jnp.float32)
    middle = rest.astype(jnp.bfloat16)
    low = (rest - middle.astype(jnp.float32)).astype(jnp.bfloat16)
    return jnp.concatenate([high, middle, low], axis=0)


def kernel(
    parts,
    splits,
    x_ref,
    mass_ref,
    stiff_ref,
    nodes_ref,
    rigid_ref,
    rows_ref,
    spring_ref,
    low_ref,
    top_ref,
    out_ref,
    value_ref,
    first_ref,
    link_ref,
    diag_ref,
    hot_ref,
    force_ref,
    send_buf,
    recv_buf,
    cols_ref,
    sum_ref,
    half_ref,
    piece_ref,
    all_ref,
    gram_ref,
    inv_ref,
    ex_send,
    ex_recv,
    quarter_send,
    quarter_recv,
    travel_send,
    travel_recv,
    fold_send,
    fold_recv,
    piece_send,
    piece_recv,
    give_send,
    give_recv,
    grow_send,
    grow_recv,
    relay_send,
    relay_recv,
):
    me = lax.axis_index("rows")
    col = lax.axis_index("vecs")
    count, width = x_ref.shape
    slots = rows_ref.shape[2]
    total_rows = count * parts

    barrier = pltpu.get_barrier_semaphore()
    for k in range(1, splits):
        pl.semaphore_signal(
            barrier, inc=1, device_id=(me, lax.rem(col + k, splits)), device_id_type=MESH
        )

    def greet(k, carry):
        pl.semaphore_signal(
            barrier, inc=1, device_id=(lax.rem(me + k, parts), col), device_id_type=MESH
        )
        return carry

    lax.fori_loop(1, parts, greet, 0)
    pl.semaphore_wait(barrier, parts - 1 + splits - 1)

    top = jnp.full((1, width), top_ref[0], jnp.float32)
    bottom = jnp.full((1, width), low_ref[0], jnp.float32)
    center = (top + bottom) * 0.5
    inverse_half = 1.0 / ((top - bottom) * 0.5)

    chunk = count // splits
    zero_pad = jnp.zeros((PAD, width), jnp.float32)
    for ref in (value_ref, first_ref, link_ref):
        ref[0:PAD, :] = zero_pad
        ref[PAD + count :, :] = zero_pad
    for lo in range(0, count, chunk):
        value_ref[PAD + lo : PAD + lo + chunk, :] = x_ref[lo : lo + chunk, :].astype(jnp.float32)

    def remote(turn, k, target):
        return pltpu.make_async_remote_copy(
            src_ref=send_buf.at[turn, target],
            dst_ref=recv_buf.at[turn, me],
            send_sem=ex_send.at[turn, k],
            recv_sem=ex_recv.at[turn, k],
            device_id=(target, col),
            device_id_type=MESH,
        )

    def arrival(turn, k):
        source = lax.rem(me + parts - k, parts)
        return pltpu.make_async_remote_copy(
            src_ref=send_buf.at[turn, source],
            dst_ref=recv_buf.at[turn, source],
            send_sem=ex_send.at[turn, k],
            recv_sem=ex_recv.at[turn, k],
            device_id=(source, col),
            device_id_type=MESH,
        )

    unroll = parts <= 8

    def send_anchors(turn, ref):
        first_row = ref[PAD + CABLE_ROWS : PAD + CABLE_ROWS + 1, :]
        last_row = ref[PAD + count - 1 : PAD + count, :]
        blank = jnp.zeros((8 - slots - 2, width), jnp.float32)

        def pick(q, carry):
            picked = [
                ref[pl.ds(PAD + jnp.minimum(rows_ref[0, q, s], count - 1), 1), :] for s in range(slots)
            ]
            send_buf[turn, q] = jnp.concatenate(picked + [first_row, last_row, blank], axis=0)
            return carry

        lax.fori_loop(0, parts, pick, 0, unroll=unroll)

        def push(k, carry):
            remote(turn, k, lax.rem(me + k, parts)).start()
            return carry

        lax.fori_loop(1, parts, push, 0, unroll=unroll)
        recv_buf[turn, me] = send_buf[turn, me]

    def collect(turn, scale):
        def take(k, carry):
            arrival(turn, k).wait_recv()
            return carry

        lax.fori_loop(1, parts, take, 0, unroll=unroll)

        def pull(q, carry):
            difference = send_buf[turn, q] - recv_buf[turn, q]
            for s in range(slots):
                live = jnp.where(rows_ref[0, q, s] < count, spring_ref[0, q, s], 0.0)
                force_ref[pl.ds(q * slots + s, 1), :] = live * difference[s : s + 1, :]
            return carry

        lax.fori_loop(0, parts, pull, 0, unroll=unroll)
        before = recv_buf[turn, lax.rem(me + parts - 1, parts)]
        after = recv_buf[turn, lax.rem(me + 1, parts)]
        own = send_buf[turn, me]
        left_open = jnp.where(me > 0, rigid_ref[0], 0.0)
        right_open = jnp.where(me < parts - 1, rigid_ref[0], 0.0)
        edge = jnp.concatenate(
            [
                left_open * (own[slots : slots + 1] - before[slots + 1 : slots + 2]),
                right_open * (own[slots + 1 : slots + 2] - after[slots : slots + 1]),
                jnp.zeros((6, width), jnp.float32),
            ],
            axis=0,
        )
        force_ref[parts * slots : parts * slots + 8, :] = edge
        return split_three(force_ref[...] * scale)

    send_anchors(0, value_ref)

    forces = force_ref.shape[0]
    order = lax.rem(lax.broadcasted_iota(jnp.int32, (1, 3 * forces), 1), forces)
    ends = parts * slots
    target = jnp.where(order == ends, CABLE_ROWS, jnp.where(order == ends + 1, count - 1, count))

    def place_anchor(q, carry):
        for s in range(slots):
            carry = jnp.where(order == q * slots + s, rows_ref[0, q, s], carry)
        return carry

    target = lax.fori_loop(0, parts, place_anchor, target, unroll=unroll)

    lane = lax.broadcasted_iota(jnp.int32, (1, width), 1)
    rigid = rigid_ref[0]
    cuts = []
    running = nodes_ref[0, 0]
    for j in range(1, nodes_ref.shape[1]):
        cuts.append(running)
        running = running + nodes_ref[0, j]
    cuts.append(running)
    for r in range(count // width):
        place = lane + r * width
        open_link = place < CABLE_ROWS - 1
        for cut in cuts:
            open_link = open_link & (place + 1 != cut)
        deck_link = (place >= CABLE_ROWS) & (place < count - 1)
        link = jnp.where(open_link, stiff_ref[r : r + 1, :], jnp.where(deck_link, rigid, 0.0))
        lo = PAD + r * width
        link_ref[lo : lo + width, :] = jnp.broadcast_to(link, (width, width)).T
        mass = mass_ref[r : r + 1, :] - center
        diag_ref[r * width : (r + 1) * width, :] = jnp.broadcast_to(mass, (width, width)).T

    def base(ref, lo):
        at = PAD + lo
        here = ref[at : at + chunk, :]
        down = link_ref[at : at + chunk, :] * (here - ref[at + 1 : at + chunk + 1, :])
        up = link_ref[at - 1 : at + chunk - 1, :] * (here - ref[at - 1 : at + chunk - 1, :])
        return diag_ref[lo : lo + chunk, :] * here + down + up

    for lo in range(0, count, chunk):
        first_ref[PAD + lo : PAD + lo + chunk, :] = base(value_ref, lo) * inverse_half
        node = lax.broadcasted_iota(jnp.int32, (chunk, 3 * forces), 0) + lo
        hot_ref[lo : lo + chunk, :] = jnp.where(node == target, 1.0, 0.0).astype(jnp.bfloat16)

    pulls = collect(0, inverse_half)
    for lo in range(0, count, chunk):
        first_ref[PAD + lo : PAD + lo + chunk, :] += jnp.dot(
            hot_ref[lo : lo + chunk, :], pulls, preferred_element_type=jnp.float32
        )
    send_anchors(1, first_ref)
    double = 2.0 * inverse_half
    for lo in range(0, count, chunk):
        diag_ref[lo : lo + chunk, :] = (
            base(first_ref, lo) * double - value_ref[PAD + lo : PAD + lo + chunk, :]
        )
    pulls = collect(1, double)
    for lo in range(0, count, chunk):
        cols_ref[col, lo : lo + chunk, :] = (
            diag_ref[lo : lo + chunk, :]
            + jnp.dot(hot_ref[lo : lo + chunk, :], pulls, preferred_element_type=jnp.float32)
        ).astype(jnp.bfloat16)

    def share(owner, target, piece, k):
        rows = pl.ds(pl.multiple_of(piece * chunk, chunk), chunk)
        return pltpu.make_async_remote_copy(
            src_ref=cols_ref.at[owner, rows],
            dst_ref=cols_ref.at[owner, rows],
            send_sem=quarter_send.at[k],
            recv_sem=quarter_recv.at[k],
            device_id=(me, target),
            device_id_type=MESH,
        )

    for k in range(1, splits):
        target = lax.rem(col + k, splits)
        share(col, target, target, k).start()
    for k in range(1, splits):
        share(lax.rem(col + splits - k, splits), col, col, k).wait_recv()

    mine = pl.ds(pl.multiple_of(col * chunk, chunk), chunk)
    packed = jnp.concatenate([cols_ref[b, mine, :] for b in range(splits)], axis=1)
    for i in range(splits):
        rows = lax.dot_general(
            packed[:, i * width : (i + 1) * width],
            packed[:, : (i + 1) * width],
            (((0,), (0,)), ((), ())),
            preferred_element_type=jnp.float32,
        )
        for j in range(i + 1):
            at = (i * (i + 1) // 2 + j) * width
            sum_ref[at : at + width, :] = rows[:, j * width : (j + 1) * width]
    length = sum_ref.shape[0]
    used = splits * (splits + 1) // 2 * width
    if used < length:
        sum_ref[used:, :] = jnp.zeros((length - used, width), jnp.float32)

    bits = splits.bit_length() - 1
    start = 0
    offset = 0
    for b in range(bits):
        half = length >> (b + 1)
        bit = lax.rem(col // (1 << b), 2)
        partner = col + (1 << b) * (1 - 2 * bit)
        landing = half_ref.at[pl.ds(offset, half)]
        copy = pltpu.make_async_remote_copy(
            src_ref=sum_ref.at[pl.ds(pl.multiple_of(start + (1 - bit) * half, 8), half)],
            dst_ref=landing,
            send_sem=fold_send.at[b],
            recv_sem=fold_recv.at[b],
            device_id=(me, partner),
            device_id_type=MESH,
        )
        copy.start()
        copy.wait()
        start = pl.multiple_of(start + bit * half, 8)
        sum_ref[pl.ds(start, half), :] += half_ref[offset : offset + half, :]
        offset += half
    part = length // splits
    unit = part // parts

    def piece(q):
        return pl.ds(pl.multiple_of(start + q * unit, 8), unit)

    def send_piece(k, carry):
        target = lax.rem(me + k, parts)
        pltpu.make_async_remote_copy(
            src_ref=sum_ref.at[piece(target)],
            dst_ref=piece_ref.at[me],
            send_sem=piece_send.at[k],
            recv_sem=piece_recv.at[k],
            device_id=(target, col),
            device_id_type=MESH,
        ).start()
        return carry

    def piece_copy(k):
        source = lax.rem(me + parts - k, parts)
        return pltpu.make_async_remote_copy(
            src_ref=sum_ref.at[piece(source)],
            dst_ref=piece_ref.at[source],
            send_sem=piece_send.at[k],
            recv_sem=piece_recv.at[k],
            device_id=(source, col),
            device_id_type=MESH,
        )

    lax.fori_loop(1, parts, send_piece, 0, unroll=unroll)

    def add_piece(k, total):
        piece_copy(k).wait_recv()
        return total + piece_ref[lax.rem(me + parts - k, parts)]

    all_ref[piece(me), :] = lax.fori_loop(1, parts, add_piece, sum_ref[piece(me), :], unroll=unroll)

    def give(owner, target, k):
        return pltpu.make_async_remote_copy(
            src_ref=all_ref.at[piece(owner)],
            dst_ref=all_ref.at[piece(owner)],
            send_sem=give_send.at[k],
            recv_sem=give_recv.at[k],
            device_id=(target, col),
            device_id_type=MESH,
        )

    def give_start(k, carry):
        give(me, lax.rem(me + k, parts), k).start()
        return carry

    def give_wait(k, carry):
        give(lax.rem(me + parts - k, parts), me, k).wait_recv()
        return carry

    lax.fori_loop(1, parts, give_start, 0, unroll=unroll)
    last_bit = lax.rem(col // (splits // 2), 2)
    last_partner = col + (splits // 2) * (1 - 2 * last_bit)
    across = start + (1 - 2 * last_bit) * part

    def relay(region, k):
        source = lax.rem(me + parts - k, parts)
        rows = pl.ds(pl.multiple_of(region + source * unit, 8), unit)
        return pltpu.make_async_remote_copy(
            src_ref=all_ref.at[rows],
            dst_ref=all_ref.at[rows],
            send_sem=relay_send.at[k],
            recv_sem=relay_recv.at[k],
            device_id=(me, last_partner),
            device_id_type=MESH,
        )

    relay(start, 0).start()

    def relay_start(k, carry):
        give_wait(k, carry)
        relay(start, k).start()
        return carry

    def relay_wait(k, carry):
        relay(across, k).wait_recv()
        return carry

    lax.fori_loop(1, parts, relay_start, 0, unroll=unroll)
    lax.fori_loop(0, parts, relay_wait, 0, unroll=unroll)

    def relay_end(k, carry):
        relay(across, k).wait_send()
        return carry

    start = start - last_bit * part
    grown = []
    held = 2 * part
    for b in reversed(range(bits - 1)):
        bit = lax.rem(col // (1 << b), 2)
        partner = col + (1 << b) * (1 - 2 * bit)

        def grow(at):
            rows = pl.ds(pl.multiple_of(at, 8), held)
            return pltpu.make_async_remote_copy(
                src_ref=all_ref.at[rows],
                dst_ref=all_ref.at[rows],
                send_sem=grow_send.at[b],
                recv_sem=grow_recv.at[b],
                device_id=(me, partner),
                device_id_type=MESH,
            )

        copy = grow(start)
        copy.start()
        grown.append(copy)
        grow(start + (1 - 2 * bit) * held).wait_recv()
        start = start - bit * held
        held = 2 * held

    first_trips, second_trips = travel_plan(splits)

    def trip(number):
        _, target, block, piece = (first_trips + second_trips)[number]
        rows = pl.ds(piece * chunk, chunk)
        return pltpu.make_async_remote_copy(
            src_ref=cols_ref.at[block, rows],
            dst_ref=cols_ref.at[block, rows],
            send_sem=travel_send.at[number],
            recv_sem=travel_recv.at[number],
            device_id=(me, target),
            device_id_type=MESH,
        )

    def each_trip(numbers, end, act):
        trips = first_trips + second_trips
        for device in range(splits):
            own = [n for n in numbers if trips[n][end] == device]
            if own:

                @pl.when(col == device)
                def _():
                    for n in own:
                        act(trip(n))

    early = range(len(first_trips))
    late = range(len(first_trips), len(first_trips) + len(second_trips))
    each_trip(early, 0, lambda copy: copy.start())

    def pass_on():
        each_trip(early, 1, lambda copy: copy.wait_recv())
        each_trip(late, 0, lambda copy: copy.start())

    for i in range(splits):
        for j in range(i + 1):
            at = (i * (i + 1) // 2 + j) * width
            gram_ref[i * width : (i + 1) * width, j * width : (j + 1) * width] = all_ref[
                at : at + width, :
            ] * (1.0 / total_rows)
    inverse_factor(gram_ref, inv_ref, pass_on)
    each_trip(late, 1, lambda copy: copy.wait_recv())

    for device in range(splits):

        @pl.when(col == device)
        def _():
            used_width = (device + 1) * width
            factor = inv_ref[device * width : used_width, :used_width].astype(jnp.bfloat16)
            for lo in range(0, count, chunk):
                block = jnp.concatenate(
                    [cols_ref[b, lo : lo + chunk, :] for b in range(device + 1)], axis=1
                )
                out_ref[lo : lo + chunk, :] = lax.dot_general(
                    block, factor, (((1,), (1,)), ((), ())), preferred_element_type=jnp.float32
                ).astype(jnp.bfloat16)

    for k in range(1, splits):
        target = lax.rem(col + k, splits)
        share(col, target, target, k).wait_send()
    each_trip(range(len(first_trips) + len(second_trips)), 0, lambda copy: copy.wait_send())
    for copy in grown:
        copy.wait_send()

    def settle(k, carry):
        target = lax.rem(me + k, parts)
        remote(0, k, target).wait_send()
        remote(1, k, target).wait_send()
        piece_copy(k).wait_send()
        give(me, target, k).wait_send()
        return carry

    lax.fori_loop(1, parts, settle, 0, unroll=unroll)
    lax.fori_loop(0, parts, relay_end, 0, unroll=unroll)


def body(
    parts,
    splits,
    vectors,
    node_mass,
    cable_stiff,
    cable_nodes,
    deck_rigidity,
    anchor_rows,
    anchor_stiff,
    cut_low,
    top_bound,
):
    count, width = vectors.shape
    slots = anchor_rows.shape[2]
    forces = parts * slots + 8
    trips = sum(len(trips) for trips in travel_plan(splits))
    size = splits * width
    blocks = splits * (splits + 1) // 2
    unit = -(-(blocks * width) // (splits * parts * 8)) * 8
    length = unit * parts * splits
    bits = splits.bit_length() - 1
    vmem = pl.BlockSpec(memory_space=pltpu.VMEM)
    smem = pl.BlockSpec(memory_space=pltpu.SMEM)
    sem = pltpu.SemaphoreType.DMA
    f32 = jnp.float32
    return pl.pallas_call(
        functools.partial(kernel, parts, splits),
        out_shape=jax.ShapeDtypeStruct((count, width), jnp.bfloat16),
        in_specs=[vmem, vmem, vmem, smem, smem, smem, smem, smem, smem],
        out_specs=vmem,
        scratch_shapes=[
            pltpu.VMEM((count + 2 * PAD, width), f32),
            pltpu.VMEM((count + 2 * PAD, width), f32),
            pltpu.VMEM((count + 2 * PAD, width), f32),
            pltpu.VMEM((count, width), f32),
            pltpu.VMEM((count, 3 * forces), jnp.bfloat16),
            pltpu.VMEM((forces, width), f32),
            pltpu.VMEM((2, parts, 8, width), f32),
            pltpu.VMEM((2, parts, 8, width), f32),
            pltpu.VMEM((splits, count, width), jnp.bfloat16),
            pltpu.VMEM((length, width), f32),
            pltpu.VMEM((length, width), f32),
            pltpu.VMEM((parts, unit, width), f32),
            pltpu.VMEM((length, width), f32),
            pltpu.VMEM((size, size), f32),
            pltpu.VMEM((size, size), f32),
            sem((2, parts)),
            sem((2, parts)),
            sem((splits,)),
            sem((splits,)),
            sem((trips,)),
            sem((trips,)),
            sem((bits,)),
            sem((bits,)),
            sem((parts,)),
            sem((parts,)),
            sem((parts,)),
            sem((parts,)),
            sem((bits,)),
            sem((bits,)),
            sem((parts,)),
            sem((parts,)),
        ],
        compiler_params=pltpu.CompilerParams(
            collective_id=0, has_side_effects=True, vmem_limit_bytes=60 * 1024 * 1024
        ),
    )(
        vectors,
        node_mass.reshape(-1, width),
        cable_stiff.reshape(-1, width),
        cable_nodes,
        deck_rigidity.reshape(1),
        anchor_rows,
        anchor_stiff,
        cut_low.reshape(1),
        top_bound.reshape(1),
    )


def solution(mesh):
    return jax.shard_map(
        functools.partial(body, mesh.shape["rows"], mesh.shape["vecs"]),
        mesh=mesh,
        in_specs=(
            P("rows", "vecs"),
            P("rows"),
            P("rows"),
            P("rows", None),
            P(),
            P("rows", None, None),
            P("rows", None, None),
            P(),
            P(),
        ),
        out_specs=P("rows", "vecs"),
        check_vma=False,
    )
```
